32 devices in a mesh: groups: 2 (over y), loans: 4 (over z), paths: 4 (over x, core).
Axes of the slice: x: 2, y: 2, z: 4, core: 2. Of those that a mesh axis runs over, the one named last changes fastest.
Arguments:
- loan_features: bfloat16 [8192, 128], P(('groups', 'loans')), parts along dimension 0, may hold values from -6 to 6
- hazard_coef: bfloat16 [128, 2], replicated, may hold values from -0.5 to 0.5
- coupon: float32 [8192], P(('groups', 'loans')), parts along dimension 0, may hold values from 0.03 to 0.075
- balance: float32 [8192], P(('groups', 'loans')), parts along dimension 0, may hold values from 0.25 to 4
- loan_term: int32 [8192], P(('groups', 'loans')), parts along dimension 0, may hold values from 180 to 360
- loan_age: int32 [8192], P(('groups', 'loans')), parts along dimension 0, may hold values from 0 to 119
- loan_region: int32 [8192], P(('groups', 'loans')), parts along dimension 0, may hold values from 0 to 415
- loan_deal: int32 [8192], P(('groups', 'loans')), parts along dimension 0, may hold values from 0 to 31, as said below
- region_hpi: float32 [832, 6, 512], P(('groups', 'loans'), None, 'paths'), parts along dimension 0, may hold values from -0.6 to 0.6
- rate_paths: float32 [2, 6, 1024], P(None, None, ('groups', 'paths')), parts along dimension 2, may hold values from 0.01 to 0.08
- deal_owner: int32 [64, 1], P('groups'), parts along dimension 0, may hold values from 0 to 3; in each aligned block of 32 rows (0 to 31, 32 to 63, ...) at most 24 rows name the same one
- tranche_order: int32 [64, 64], P('groups'), parts along dimension 0, may hold values from 0 to 63, each once within a row
- tranche_share: float32 [64, 64], P('groups'), parts along dimension 0, may hold values from 0.2 to 5
- tranche_rate: float32 [64, 64], P('groups'), parts along dimension 0, may hold values from 0.02 to 0.07
Outputs:
- tranche_value: float32 [64, 64], P('groups'), parts along dimension 0
The draws below stay inside these ranges and needn't reach their ends.
There are 2 independent parts, one for each index of `groups`. The reference program is written for one: setup_inputs(seed, part) draws one part's arguments, and reference() takes and returns one part's arrays. A program takes and returns all parts, laid end to end along the dimension named above; an argument that names none is the same for every part. Nothing has to cross between parts.
Inputs may be any that keep to these rules, and one draw needn't show every extreme that they name: `loan_deal`: every deal holds at least one loan. `deal_owner`: no index of loans owns more than 24 deals, and one owns exactly 24. `tranche_order`: each row names every tranche once.
All inputs are finite; a program needn't handle non-finite values.
Results may differ from the reference program's by a relative error of at most 0.0003.
Values sent between devices are 32-bit elements; how exact they have to be, the bound alone decides.
A program may use at most 64 MiB of HBM per device.

```python
import math
import jax
import jax.numpy as jnp
import numpy as np
from jax import lax

PATH_DEV = 128
STEPS = 6
REGIONS = 416
TRANCHES = 64
FEAT = 128
DEAL_MAX = 24
LOANS = 4096
PATHS = 512
DEALS = 32
N_LOANS = 4
N_PATHS = 4


def draw_loan_deal(key, part):
    first, second = jax.random.split(jax.random.fold_in(key, 11))
    picks = jax.random.randint(first, (LOANS,), 0, DEALS).astype(jnp.int32)
    spots = jax.random.permutation(second, LOANS)[:DEALS]
    return picks.at[spots].set(jnp.arange(DEALS, dtype=jnp.int32)).astype(jnp.int32)


def set_ends(result, own_key, low, high):
    longest = result.shape.index(max(result.shape))
    spots = []
    for shift in (0, 1):
        where = [jax.random.randint(jax.random.fold_in(own_key, axis), (), 0, length) for axis, length in enumerate(result.shape)]
        where[longest] = (where[longest] + shift) % result.shape[longest]
        spots.append(tuple(where))
    return result.at[spots[0]].set(low).at[spots[1]].set(high)


def levels(rng, extent, cuts, least, top_value):
    def one(position, blocks):
        heights = jax.random.uniform(jax.random.fold_in(jax.random.fold_in(rng, 6), position), (blocks,), jnp.float32, least / len(cuts), top_value / len(cuts))
        return jnp.repeat(jnp.exp(heights), extent[position] // blocks).reshape((-1,) + (1,) * (len(extent) - position - 1))

    level = one(*cuts[0])
    for cut in cuts[1:]:
        level = level * one(*cut)
    return level


def rank_bounds(count, lean):
    weights = [(1 << 20) // math.isqrt(grade ** lean) + 1 for grade in range(1, count + 1)]
    deviation = 1 + sum(weights) // (1 << 30)
    return np.cumsum(np.array([max(1, weight // deviation) for weight in weights]))


def ranked(own_key, dims, amount, skew):
    table = rank_bounds(amount, skew)
    ticket = jax.random.randint(jax.random.fold_in(own_key, 1), dims, 0, int(table[amount - 1]))
    grade = jnp.searchsorted(jnp.asarray(table, jnp.int32), ticket, side="right")
    return jax.random.permutation(jax.random.fold_in(own_key, 2), amount)[grade].astype(jnp.int32)


def shared_out(key, own, number, rows, number_of, top, limit, slope):
    ranking = jax.random.permutation(key, number_of)
    crowded, common = load_shares(number_of, rows * top, limit, slope, True), load_shares(number_of, rows * top, limit, slope, False)
    places = jnp.arange(number_of)

    def named(tallies, rotation):
        used = int((tallies > 0).sum())
        fixed = max(1, used // 4)
        shifted = fixed + (places - fixed + rotation * (used - fixed)) % max(1, number_of - fixed)
        return jnp.zeros((number_of,), jnp.int32).at[ranking[jnp.where(places < fixed, places, shifted)]].set(jnp.asarray(tallies, jnp.int32))

    tallies = jnp.where(number % 4 == 0, named(crowded, number // 4), named(common, number - number // 4 - 1))
    mixed = jax.random.permutation(jax.random.fold_in(own, 3), number_of)
    source_of, taker = mixed[0:number_of // 2 * 2:2], mixed[1:number_of // 2 * 2:2]
    margin = jnp.minimum(tallies[source_of] - 1, limit - tallies[taker]) // 2
    margin = jnp.where((source_of == ranking[0]) | (taker == ranking[0]) | (tallies[taker] == 0), 0, jnp.maximum(margin, 0))
    shifted = jax.random.randint(jax.random.fold_in(own, 4), (number_of // 2,), 0, 1 << 20) % (margin + 1)
    tallies = tallies.at[source_of].add(-shifted).at[taker].add(shifted)
    items = jnp.searchsorted(jnp.cumsum(tallies), jnp.arange(rows * top), side="right").astype(jnp.int32)
    table = items.reshape(top, rows).T
    table = table[jax.random.permutation(jax.random.fold_in(own, 1), rows)]
    rotation = jax.random.randint(jax.random.fold_in(own, 2), (rows, 1), 0, top)
    return jnp.take_along_axis(table, (jnp.arange(top)[None, :] + rotation) % top, axis=1)


def load_shares(number_of, total, bound, lean, full):
    weights = [(1 << 20) // math.isqrt(grade ** lean) + 1 for grade in range(1, number_of + 1)]
    largest = bound if full else min(bound, max(-(-total // number_of), total * weights[0] // sum(weights)))
    least = 1 if total - largest >= number_of - 1 else 0
    holding, rest = [largest] + [least] * (number_of - 1), total - largest - least * (number_of - 1)
    while rest > 0:
        candidates = [i for i in range(1, number_of) if holding[i] < largest] or [i for i in range(1, number_of) if holding[i] < bound]
        pool, remaining = sum([weights[i] for i in candidates]), rest
        for i in candidates:
            addition = min(bound - holding[i], max(1, remaining * weights[i] // pool), rest)
            holding[i] = holding[i] + addition
            rest = rest - addition
    return np.array(holding)


def gaussian(stream_key, extent, scale, reach, pieces=(), kind=jnp.bfloat16):
    result = jax.random.normal(stream_key, extent, jnp.float32) * scale
    if len(pieces) > 0:
        result = levels(stream_key, extent, pieces, -0.22, 0.18) * result
    return jnp.clip(result, min=-reach, max=reach).astype(kind)


def setup_inputs(seed: int = 0, part: int = 0) -> dict:
    splits = jax.random.split(jax.random.key(seed), 15)
    part_splits = jax.random.split(jax.random.fold_in(splits[14], part), 15)
    loan_features = gaussian(part_splits[0], (LOANS, FEAT), 1.0, 6.0, ((0, 4),))
    hazard_coef = gaussian(splits[1], (FEAT, 2), FEAT ** -0.5, 0.5)
    coupon = jnp.clip(0.03 + 0.045 * jax.random.uniform(part_splits[2], (LOANS,), jnp.float32) ** levels(part_splits[2], (LOANS,), ((0, 4),), -0.2, 0.2), 0.03, 0.075)
    balance = jnp.clip(jnp.exp(math.log(4.0) - 2.7725887 * jax.random.uniform(part_splits[3], (LOANS,), jnp.float32) ** levels(part_splits[3], (LOANS,), ((0, 4),), -0.2, 0.2)), 0.25, 4.0)
    loan_term = set_ends(jax.random.randint(part_splits[4], (LOANS,), 180, 361), jax.random.fold_in(part_splits[4], 1), 180, 360).astype(jnp.int32)
    loan_age = set_ends(jax.random.randint(part_splits[5], (LOANS,), 0, 120), jax.random.fold_in(part_splits[5], 1), 0, 119).astype(jnp.int32)
    loan_region = set_ends(ranked(part_splits[6], (LOANS,), REGIONS, 2), jax.random.fold_in(part_splits[6], 3), 0, REGIONS - 1).astype(jnp.int32)
    loan_deal = draw_loan_deal(jax.random.fold_in(jax.random.fold_in(splits[14], part), 71), part)
    region_hpi = gaussian(part_splits[8], (REGIONS, STEPS, PATHS), 0.15, 0.6, ((0, 4), (2, 4)), jnp.float32)
    rate_paths = jnp.clip(0.01 + 0.07 * jax.random.uniform(part_splits[9], (2, STEPS, PATHS), jnp.float32) ** levels(part_splits[9], (2, STEPS, PATHS), ((2, 4),), -0.2, 0.2), 0.01, 0.08)
    deal_owner_keys = jax.random.split(jax.random.fold_in(part_splits[10], 1), DEALS // DEALS)
    deal_owner_turns = jax.random.permutation(jax.random.fold_in(part_splits[10], 3), DEALS // DEALS)
    deal_owner = jax.vmap(lambda own, number: shared_out(jax.random.fold_in(part_splits[10], 2), own, number, DEALS, N_LOANS, 1, DEAL_MAX, 2))(deal_owner_keys, deal_owner_turns).reshape((DEALS, 1))
    tranche_order = jax.vmap(lambda own: jax.random.permutation(own, TRANCHES))(jax.random.split(part_splits[11], DEALS)).reshape((DEALS, TRANCHES)).astype(jnp.int32)
    tranche_share = jnp.clip(jnp.exp(jax.random.uniform(part_splits[12], (DEALS, TRANCHES), jnp.float32, math.log(0.2), math.log(5.0))), 0.2, 5.0)
    tranche_rate = jnp.clip(jax.random.uniform(part_splits[13], (DEALS, TRANCHES), jnp.float32, 0.02, 0.07), 0.02, 0.07)
    return dict(loan_features=loan_features, hazard_coef=hazard_coef, coupon=coupon, balance=balance, loan_term=loan_term, loan_age=loan_age, loan_region=loan_region, loan_deal=loan_deal, region_hpi=region_hpi, rate_paths=rate_paths, deal_owner=deal_owner, tranche_order=tranche_order, tranche_share=tranche_share, tranche_rate=tranche_rate)


prepay_base = -4.0
incentive = 40.0
default_base = -6.0
price_sens = 12.0
oas_spread = 0.005


def loan_month(held, covar, coupon, rate_month, sched_rate, mortgage_now, hpi_now):
    smm = jax.nn.sigmoid(covar[:, 0][None, :] + prepay_base + incentive * (coupon[None, :] - mortgage_now[:, None]))
    mdr = jax.nn.sigmoid(covar[:, 1][None, :] + default_base - price_sens * hpi_now)
    interest = held * rate_month[None, :]
    sched = held * sched_rate[None, :]
    lost = mdr * held
    prepaid = smm * (held - sched - lost)
    principal = sched + prepaid + lost
    return held - principal, principal, interest


def priority_mask(tranche_order):
    count = tranche_order.shape[1]
    spots = jnp.arange(count, dtype=jnp.int32)
    hits = tranche_order[:, :, None] == spots[None, None, :]
    prio = jnp.sum(jnp.where(hits, spots[None, :, None], 0), axis=1)
    return (prio[:, :, None] < prio[:, None, :]).astype(jnp.float32)


def waterfall(princ, inter, starts, shares, rates, ahead_mask, short, valid):
    steps = princ.shape[2]
    blank = 1.0 - valid
    weights = shares / (jnp.sum(shares, axis=1, keepdims=True) + blank[:, None])
    opening = weights * starts[:, None]
    safe_open = opening + blank[:, None]
    held = jnp.broadcast_to(opening[:, None, :], (princ.shape[0], princ.shape[1], shares.shape[1]))
    decay = jnp.exp(-jnp.cumsum(short + oas_spread, axis=0) / 12.0)
    worth = jnp.zeros_like(held)
    for step in range(steps):
        ahead = jnp.einsum("xpj,xjk->xpk", held, ahead_mask, precision=lax.Precision.HIGHEST)
        paid = jnp.minimum(jnp.maximum(princ[:, :, step, None] - ahead, 0.0), held)
        coupon_due = rates[:, None, :] * held
        denom = jnp.sum(coupon_due, axis=2, keepdims=True) + blank[:, None, None]
        flow = paid + inter[:, :, step, None] * coupon_due / denom
        worth = worth + flow * decay[step][None, :, None]
        held = held - paid
    worth = worth + held * decay[steps - 1][None, :, None]
    return jnp.sum(worth / safe_open[:, None, :], axis=1)


def reference(loan_features, hazard_coef, coupon, balance, loan_term, loan_age, loan_region, loan_deal, region_hpi, rate_paths, deal_owner, tranche_order, tranche_share, tranche_rate):
    covar = jnp.dot(loan_features, hazard_coef, preferred_element_type=jnp.float32)
    rate_month = coupon / 12.0
    term_left = (loan_term - loan_age).astype(jnp.float32)
    hpi_blocks = region_hpi.reshape(REGIONS, STEPS, N_PATHS, PATH_DEV).transpose(2, 0, 1, 3)
    mort_blocks = rate_paths[1].reshape(STEPS, N_PATHS, PATH_DEV).transpose(1, 0, 2)

    def one_block(pair):
        hpi_block, mort_block = pair
        held = jnp.broadcast_to(balance[None, :], (PATH_DEV, LOANS))
        sums = []
        for step in range(STEPS):
            sched_rate = rate_month / jnp.expm1((term_left - step) * jnp.log1p(rate_month))
            hpi_now = jnp.take(hpi_block[:, step, :], loan_region, axis=0).T
            held, principal, interest = loan_month(held, covar, coupon, rate_month, sched_rate, mort_block[step], hpi_now)
            prin_deal = jax.ops.segment_sum(principal.T, loan_deal, num_segments=DEALS)
            int_deal = jax.ops.segment_sum(interest.T, loan_deal, num_segments=DEALS)
            sums.append(jnp.stack([prin_deal, int_deal], 1))
        return jnp.stack(sums, 3)

    flows = lax.map(one_block, (hpi_blocks, mort_blocks))
    flows = flows.transpose(1, 2, 0, 3, 4).reshape(DEALS, 2, PATHS, STEPS)
    starts = jax.ops.segment_sum(balance, loan_deal, num_segments=DEALS)
    ahead_mask = priority_mask(tranche_order)
    total = waterfall(flows[:, 0], flows[:, 1], starts, tranche_share, tranche_rate, ahead_mask, rate_paths[0], jnp.ones((DEALS,), jnp.float32))
    value = 100.0 * (total / PATHS - 1.0)
    order_key = deal_owner[:, 0] * DEALS + jnp.arange(DEALS, dtype=jnp.int32)
    listing = jnp.argsort(order_key)
    return value[listing]
```

```python
import functools

import jax
import jax.numpy as jnp
from jax import lax
from jax.experimental import pallas as pl
from jax.experimental.pallas import tpu as pltpu
from jax.sharding import PartitionSpec as P

prepay_base = -4.0
incentive = 40.0
default_base = -6.0
price_sens = 12.0
oas_spread = 0.005
CHUNK = 512


def loan_month(held, covar, coupon, rate_month, sched_rate, mortgage_now, hpi_now):
    smm = jax.nn.sigmoid(
        covar[:, 0][None, :] + prepay_base + incentive * (coupon[None, :] - mortgage_now[:, None])
    )
    mdr = jax.nn.sigmoid(covar[:, 1][None, :] + default_base - price_sens * hpi_now)
    interest = held * rate_month[None, :]
    sched = held * sched_rate[None, :]
    lost = mdr * held
    prepaid = smm * (held - sched - lost)
    principal = sched + prepaid + lost
    return (held - principal, principal, interest)


def priority_mask(tranche_order):
    count = tranche_order.shape[1]
    spots = jnp.arange(count, dtype=jnp.int32)
    hits = tranche_order[:, :, None] == spots[None, None, :]
    prio = jnp.sum(jnp.where(hits, spots[None, :, None], 0), axis=1)
    return (prio[:, :, None] < prio[:, None, :]).astype(jnp.float32)


def waterfall(princ, inter, starts, shares, rates, ahead_mask, short, valid):
    steps = princ.shape[2]
    blank = 1.0 - valid
    weights = shares / (jnp.sum(shares, axis=1, keepdims=True) + blank[:, None])
    opening = weights * starts[:, None]
    safe_open = opening + blank[:, None]
    held = jnp.broadcast_to(opening[:, None, :], (princ.shape[0], princ.shape[1], shares.shape[1]))
    decay = jnp.exp(-jnp.cumsum(short + oas_spread, axis=0) / 12.0)
    worth = jnp.zeros_like(held)
    for step in range(steps):
        ahead = jnp.einsum("xpj,xjk->xpk", held, ahead_mask, precision=lax.Precision.HIGHEST)
        paid = jnp.minimum(jnp.maximum(princ[:, :, step, None] - ahead, 0.0), held)
        coupon_due = rates[:, None, :] * held
        denom = jnp.sum(coupon_due, axis=2, keepdims=True) + blank[:, None, None]
        flow = paid + inter[:, :, step, None] * coupon_due / denom
        worth = worth + flow * decay[step][None, :, None]
        held = held - paid
    worth = worth + held * decay[steps - 1][None, :, None]
    return jnp.sum(worth / safe_open[:, None, :], axis=1)


def on_device(
    loan_features,
    hazard_coef,
    coupon,
    balance,
    loan_term,
    loan_age,
    loan_region,
    loan_deal,
    region_hpi,
    rate_paths,
    deal_owner,
    tranche_order,
    tranche_share,
    tranche_rate,
):
    highest = lax.Precision.HIGHEST
    loans_here = coupon.shape[0]
    paths_here = rate_paths.shape[2]
    steps = rate_paths.shape[1]
    deals = deal_owner.shape[0]
    groups = lax.axis_size("loans")
    me_loan = lax.axis_index("loans")
    covar = jnp.dot(loan_features, hazard_coef, preferred_element_type=jnp.float32)
    piece = lax.all_gather(region_hpi, "loans", axis=0, tiled=True)
    rows = piece.shape[0]
    marks = (loan_region[None, :] == lax.iota(jnp.int32, rows)[:, None]).astype(jnp.float32)
    loan_hpi = jnp.einsum("rc,rl->cl", piece.reshape(rows, -1), marks, precision=highest)
    loan_hpi = loan_hpi.reshape(steps, paths_here, loans_here)
    rate_month = coupon / 12.0
    term_left = (loan_term - loan_age).astype(jnp.float32)
    held = jnp.broadcast_to(balance[None, :], (paths_here, loans_here))
    prin_list = []
    int_list = []
    for step in range(steps):
        sched_rate = rate_month / jnp.expm1((term_left - step) * jnp.log1p(rate_month))
        held, principal, interest = loan_month(
            held, covar, coupon, rate_month, sched_rate, rate_paths[1, step], loan_hpi[step]
        )
        prin_list.append(principal)
        int_list.append(interest)
    cash = jnp.stack([jnp.stack(prin_list, 1), jnp.stack(int_list, 1)], 1)
    deal_ids = lax.iota(jnp.int32, deals)
    match = loan_deal[:, None] == deal_ids[None, :]
    onehot_deal = match.astype(jnp.float32)
    totals = lax.psum(jnp.dot(balance, onehot_deal, precision=highest), "loans")
    owners = deal_owner[:, 0]
    order_key = owners * deals + deal_ids
    position = jnp.sum((order_key[None, :] < order_key[:, None]).astype(jnp.int32), axis=1)
    place = (position[None, :] == deal_ids[:, None]).astype(jnp.float32)
    ahead_mask = priority_mask(tranche_order)
    portion = paths_here // groups
    block = cash.reshape(-1, loans_here)
    path_flows = lax.psum_scatter(
        jnp.dot(block, onehot_deal, precision=highest).reshape(
            portion * lax.axis_size("loans"), 2, steps, deals
        ),
        "loans",
        scatter_dimension=0,
        tiled=True,
    )
    flows = path_flows.transpose(3, 0, 1, 2)
    short = lax.dynamic_slice_in_dim(rate_paths[0], me_loan * portion, portion, 1)
    by_deal = waterfall(
        flows[:, :, 0, :],
        flows[:, :, 1, :],
        totals,
        tranche_share,
        tranche_rate,
        ahead_mask,
        short,
        jnp.ones((deals,), jnp.float32),
    )
    ordered = jnp.dot(place, by_deal, precision=highest)
    mine = lax.psum(ordered, "loans")
    total = lax.psum(mine, "paths")
    all_paths = paths_here * lax.axis_size("paths")
    return 100.0 * (total / all_paths - 1.0)


MESH = pl.DeviceIdType.MESH


def rows_of(x):
    return x.reshape((1,) + x.shape)


def pool_kernel(groups, lanes_out, chunk,
                feat, coef, coupon, balance, term, age, region, deal, hpi, rates, owner, order, share, trate,
                out,
                loan_tx, loan_rx, hpi_tx, hpi_rx, left, marks, cash, pool, table, cols, part, part_rx, half, half_rx,
                loan_ss, loan_rs, hpi_ss, hpi_rs, part_ss, part_rs, half_ss, half_rs, own_sem):
    n_loans, n_paths = groups
    f32, bf16 = jnp.float32, jnp.bfloat16
    me = lax.axis_index("loans")
    me_path = lax.axis_index("paths")
    n = coupon.shape[1]
    rows, steps, paths = hpi.shape
    here = paths // n_loans
    wide = hpi_tx.shape[2]
    deals, tranches = share.shape
    copies = lanes_out // deals

    barrier = pltpu.get_barrier_semaphore()
    for off in range(1, n_loans):
        pl.semaphore_signal(barrier, inc=1, device_id={"loans": lax.rem(me + off, n_loans)}, device_id_type=MESH)
    for off in range(1, n_paths):
        pl.semaphore_signal(barrier, inc=1, device_id={"paths": lax.rem(me_path + off, n_paths)}, device_id_type=MESH)

    covar = lax.dot_general(coef[...], feat[...], (((0,), (1,)), ((), ())), preferred_element_type=f32)
    note = coupon[...]
    place = region[...]
    place = place + (place // rows) * (wide - rows)
    loan_tx[...] = jnp.concatenate(
        [
            0.5 * (covar[0:1, :] + prepay_base + incentive * note),
            0.5 * (covar[1:2, :] + default_base),
            note / 12.0,
            balance[...],
            (term[...] - age[...]).astype(f32),
            place.astype(f32),
            deal[...].astype(f32),
            jnp.zeros((1, n), f32),
        ],
        axis=0,
    )
    for step in range(steps):
        block = hpi[:, step, :] * (-0.5 * price_sens)
        if wide > rows:
            block = jnp.concatenate([block, jnp.zeros((wide - rows, paths), f32)], axis=0)
        hpi_tx[step] = block.T

    pl.semaphore_wait(barrier, n_loans + n_paths - 2)
    loan_copies, hpi_copies = [], []
    for off in range(1, n_loans):
        there = lax.rem(me + off, n_loans)
        loan_copies.append(pltpu.make_async_remote_copy(
            src_ref=loan_tx, dst_ref=loan_rx.at[me], send_sem=loan_ss.at[off], recv_sem=loan_rs.at[off],
            device_id={"loans": there}, device_id_type=MESH))
        hpi_copies.append(pltpu.make_async_remote_copy(
            src_ref=hpi_tx.at[:, pl.ds(pl.multiple_of(there * here, here), here), :],
            dst_ref=hpi_rx.at[me], send_sem=hpi_ss.at[off], recv_sem=hpi_rs.at[off],
            device_id={"loans": there}, device_id_type=MESH))
    for copy in loan_copies:
        copy.start()
    for copy in hpi_copies:
        copy.start()
    own_loan = pltpu.make_async_copy(loan_tx, loan_rx.at[me], own_sem.at[0])
    own_hpi = pltpu.make_async_copy(
        hpi_tx.at[:, pl.ds(pl.multiple_of(me * here, here), here), :], hpi_rx.at[me], own_sem.at[1])
    own_loan.start()
    own_hpi.start()

    ids = lax.broadcasted_iota(jnp.int32, (deals, 128), 0)
    key = (jnp.broadcast_to(owner[...], (deals, 128)) * deals + ids).astype(f32)
    key_row = key.T[:deals, :]
    below = jnp.where(key[:, :deals] < key_row, 1.0, 0.0).astype(f32)
    spot = jnp.sum(below, axis=0, keepdims=True)
    perm = jnp.where(spot == lax.broadcasted_iota(jnp.int32, (deals, deals), 0).astype(f32), 1.0, 0.0).astype(f32)
    listing = jnp.sum(perm * lax.broadcasted_iota(jnp.int32, (deals, deals), 1).astype(f32), axis=1, keepdims=True)
    listing = jnp.concatenate([listing] * copies, axis=0)

    def spread(x):
        x = jnp.dot(perm, x, preferred_element_type=f32, precision=lax.Precision.HIGHEST)
        x = jnp.concatenate([x, jnp.zeros((deals, 128 - tranches), f32)], axis=1)
        return jnp.concatenate([x] * copies, axis=0).T[:tranches, :]

    table[...] = spread(order[...].astype(f32))
    share_t = spread(share[...])
    rate_t = spread(trate[...])
    names = lax.broadcasted_iota(jnp.int32, (tranches, lanes_out), 0).astype(f32)

    def walk(j, carry):
        run, upto = carry
        hit = names == table[pl.ds(j, 1), :]
        run = run + jnp.sum(jnp.where(hit, share_t, 0.0), axis=0, keepdims=True)
        return run, jnp.where(hit, run, upto)

    whole, upto = lax.fori_loop(
        0, tranches, walk, (jnp.zeros((1, lanes_out), f32), jnp.zeros((tranches, lanes_out), f32)), unroll=4)
    weight = share_t / whole
    upto = upto / whole
    per_weight = 1.0 / weight
    due_t = rate_t * weight

    stack = jnp.concatenate([rates[0], rates[1], jnp.zeros((128 - 2 * steps, paths), f32)], axis=0)
    cols[...] = stack.T
    mine = cols[pl.ds(pl.multiple_of(me * here, here), here), :]
    mort = [(0.5 * incentive) * mine[:, steps + t:steps + t + 1] for t in range(steps)]
    disc = []
    total = jnp.zeros((here, 1), f32)
    for t in range(steps):
        total = total + (mine[:, t:t + 1] + oas_spread)
        disc.append(jnp.exp(-total / 12.0))

    own_loan.wait()
    for copy in loan_copies:
        copy.wait_recv()
    ages = lax.broadcasted_iota(jnp.int32, (8, n), 0).astype(f32)
    for src in range(n_loans):
        r = loan_rx[src, 2:3, :]
        grown = 1.0 + r
        log = jnp.log(grown) * (r / (grown - 1.0))
        x = (loan_rx[src, 4:5, :] - ages) * log
        left[src] = r / (jnp.exp(x) - 1.0)
    pool[...] = jnp.zeros(pool.shape, f32)
    own_hpi.wait()
    for copy in hpi_copies:
        copy.wait_recv()
    height = steps * here
    for src in range(n_loans):
        x = hpi_rx[src].reshape(height, wide)
        high = x.astype(bf16)
        marks[0:height, src * wide:(src + 1) * wide] = high
        marks[height:2 * height, src * wide:(src + 1) * wide] = (x - high.astype(f32)).astype(bf16)

    depth = n_loans * wide
    per = n // chunk

    def work(c, _):
        src = c // per
        lane = pl.ds(pl.multiple_of((c % per) * chunk, chunk), chunk)
        lv = loan_rx[src, :, lane]
        sched_rate = left[src, :, lane]
        pick = jnp.where(
            lax.broadcasted_iota(jnp.int32, (depth, chunk), 0) == lv[5:6, :].astype(jnp.int32), 1.0, 0.0).astype(bf16)
        got = jnp.dot(marks[...], pick, preferred_element_type=f32)
        held = jnp.broadcast_to(lv[3:4, :], (here, chunk))
        r = lv[2:3, :]
        for t in range(steps):
            h = got[t * here:(t + 1) * here] + got[height + t * here:height + (t + 1) * here]
            smm = 0.5 + 0.5 * jnp.tanh(lv[0:1, :] - mort[t])
            mdr = 0.5 + 0.5 * jnp.tanh(lv[1:2, :] + h)
            interest = held * r
            sched = held * sched_rate[t:t + 1, :]
            lost = mdr * held
            principal = sched + smm * (held - sched - lost) + lost
            held = held - principal
            base = t * 4 * here
            for k, x in enumerate((principal, interest)):
                high = x.astype(bf16)
                cash[base + k * here:base + (k + 1) * here, :] = high
                cash[base + (k + 2) * here:base + (k + 3) * here, :] = (x - high.astype(f32)).astype(bf16)
        b = jnp.broadcast_to(lv[3:4, :], (16, chunk))
        high = b.astype(bf16)
        cash[4 * height:4 * height + 16, :] = high
        cash[4 * height + 16:4 * height + 32, :] = (b - high.astype(f32)).astype(bf16)
        member = jnp.where(listing == lv[6:7, :], 1.0, 0.0).astype(bf16)
        pool[...] += lax.dot_general(cash[...], member, (((1,), (1,)), ((), ())), preferred_element_type=f32)
        return 0

    lax.fori_loop(0, n_loans * per, work, 0)

    start = pool[4 * height:4 * height + 1, :] + pool[4 * height + 16:4 * height + 17, :]
    per_start = 1.0 / start
    sub = here // copies
    group = lax.broadcasted_iota(jnp.int32, (sub, lanes_out), 1) // deals

    def packed(x):
        x = jnp.broadcast_to(x, (here, lanes_out))
        y = x[0:sub]
        for c in range(1, copies):
            y = jnp.where(group == c, x[c * sub:(c + 1) * sub], y)
        return y

    paid_upto = jnp.zeros((sub, lanes_out), f32)
    gone, gains, fall = [], [], []
    for t in range(steps):
        base = t * 4 * here
        princ = packed(pool[base:base + here, :] + pool[base + 2 * here:base + 3 * here, :])
        inter = packed(pool[base + here:base + 2 * here, :] + pool[base + 3 * here:base + 4 * here, :])
        paid_upto = paid_upto + jnp.maximum(princ, 0.0)
        gone.append(paid_upto * per_start)
        gains.append(inter * per_start)
        fall.append(packed(disc[t]))
    worth = jnp.zeros((tranches, lanes_out), f32)
    for j in range(sub):
        frac = jnp.ones((tranches, lanes_out), f32)
        for t in range(steps):
            d = fall[t][j:j + 1, :]
            later = jnp.clip((upto - gone[t][j:j + 1, :]) * per_weight, 0.0, 1.0)
            denom = jnp.sum(due_t * frac, axis=0, keepdims=True)
            flow = (frac - later) + (gains[t][j:j + 1, :] / denom) * (rate_t * frac)
            worth = worth + flow * d
            frac = later
        worth = worth + frac * d
    wt = jnp.concatenate([worth, jnp.zeros((128 - tranches, lanes_out), f32)], axis=0).T
    acc = wt[0:deals]
    for c in range(1, copies):
        acc = acc + wt[c * deals:(c + 1) * deals]
    part[...] = acc
    part_copies = []
    for off in range(1, n_loans):
        part_copies.append(pltpu.make_async_remote_copy(
            src_ref=part, dst_ref=part_rx.at[me], send_sem=part_ss.at[off], recv_sem=part_rs.at[off],
            device_id={"loans": lax.rem(me + off, n_loans)}, device_id_type=MESH))
    for copy in part_copies:
        copy.start()
    part_rx[me] = acc
    for copy in part_copies:
        copy.wait_recv()
    acc = part_rx[0]
    for src in range(1, n_loans):
        acc = acc + part_rx[src]
    half[...] = acc
    half_copies = []
    for off in range(1, n_paths):
        half_copies.append(pltpu.make_async_remote_copy(
            src_ref=half, dst_ref=half_rx.at[me_path], send_sem=half_ss.at[off], recv_sem=half_rs.at[off],
            device_id={"paths": lax.rem(me_path + off, n_paths)}, device_id_type=MESH))
    for copy in half_copies:
        copy.start()
    half_rx[me_path] = acc
    for copy in half_copies:
        copy.wait_recv()
    acc = half_rx[0]
    for src in range(1, n_paths):
        acc = acc + half_rx[src]
    out[...] = (100.0 * (acc / (paths * n_paths) - 1.0))[:, :tranches]
    for copy in loan_copies + hpi_copies + part_copies + half_copies:
        copy.wait_send()


def fused(loan_features, hazard_coef, coupon, balance, loan_term, loan_age, loan_region, loan_deal,
          region_hpi, rate_paths, deal_owner, tranche_order, tranche_share, tranche_rate):
    n_loans, n_paths = lax.axis_size("loans"), lax.axis_size("paths")
    n = coupon.shape[0]
    rows, steps, paths = region_hpi.shape
    deals, tranches = tranche_share.shape
    here = paths // n_loans
    wide = -(-rows // 128) * 128
    lanes_out = 128
    chunk = min(n, CHUNK)
    height = steps * here
    f32 = jnp.float32
    dma = pltpu.SemaphoreType.DMA
    return pl.pallas_call(
        functools.partial(pool_kernel, (n_loans, n_paths), lanes_out, chunk),
        out_shape=jax.ShapeDtypeStruct((deals, tranches), f32),
        in_specs=[pl.BlockSpec(memory_space=pltpu.VMEM)] * 14,
        out_specs=pl.BlockSpec(memory_space=pltpu.VMEM),
        scratch_shapes=[
            pltpu.VMEM((8, n), f32),
            pltpu.VMEM((n_loans, 8, n), f32),
            pltpu.VMEM((steps, paths, wide), f32),
            pltpu.VMEM((n_loans, steps, here, wide), f32),
            pltpu.VMEM((n_loans, 8, n), f32),
            pltpu.VMEM((2 * height, n_loans * wide), jnp.bfloat16),
            pltpu.VMEM((4 * height + 32, chunk), jnp.bfloat16),
            pltpu.VMEM((4 * height + 32, lanes_out), f32),
            pltpu.VMEM((tranches, lanes_out), f32),
            pltpu.VMEM((paths, 128), f32),
            pltpu.VMEM((deals, 128), f32),
            pltpu.VMEM((n_loans, deals, 128), f32),
            pltpu.VMEM((deals, 128), f32),
            pltpu.VMEM((n_paths, deals, 128), f32),
            dma((n_loans,)), dma((n_loans,)), dma((n_loans,)), dma((n_loans,)),
            dma((n_loans,)), dma((n_loans,)), dma((n_paths,)), dma((n_paths,)), dma((2,)),
        ],
        compiler_params=pltpu.CompilerParams(collective_id=0, has_side_effects=True),
    )(loan_features, hazard_coef, rows_of(coupon), rows_of(balance), rows_of(loan_term), rows_of(loan_age),
      rows_of(loan_region), rows_of(loan_deal), region_hpi, rate_paths, deal_owner, tranche_order,
      tranche_share, tranche_rate)


def fits(args):
    n = args[2].shape[0]
    paths = args[8].shape[2]
    deals, tranches = args[12].shape
    n_loans = lax.axis_size("loans")
    return (
        paths == 128 and deals % 8 == 0 and 128 % deals == 0 and tranches <= 128 and tranches % 8 == 0
        and paths % (32 * n_loans) == 0 and (paths // n_loans) % (8 * (128 // deals)) == 0
        and n % min(n, CHUNK) == 0 and n % 128 == 0 and args[8].shape[0] % 8 == 0 and args[9].shape[1] <= 8
    )


def device_program(*args):
    return fused(*args) if fits(args) else on_device(*args)


def solution(mesh):
    in_specs = (
        P(("groups", "loans"), None),
        P(),
        P(("groups", "loans")),
        P(("groups", "loans")),
        P(("groups", "loans")),
        P(("groups", "loans")),
        P(("groups", "loans")),
        P(("groups", "loans")),
        P(("groups", "loans"), None, "paths"),
        P(None, None, ("groups", "paths")),
        P("groups", None),
        P("groups", None),
        P("groups", None),
        P("groups", None),
    )
    out_specs = P("groups", None)
    return jax.shard_map(
        device_program, mesh=mesh, in_specs=in_specs, out_specs=out_specs, check_vma=False
    )
```

```python
import functools

import jax
import jax.numpy as jnp
from jax import lax
from jax.experimental import pallas as pl
from jax.experimental.pallas import tpu as pltpu
from jax.sharding import PartitionSpec as P

prepay_base = -4.0
incentive = 40.0
default_base = -6.0
price_sens = 12.0
oas_spread = 0.005
EARLY = 4


def loan_month(held, covar, coupon, rate_month, sched_rate, mortgage_now, hpi_now):
    smm = jax.nn.sigmoid(
        covar[:, 0][None, :] + prepay_base + incentive * (coupon[None, :] - mortgage_now[:, None])
    )
    mdr = jax.nn.sigmoid(covar[:, 1][None, :] + default_base - price_sens * hpi_now)
    interest = held * rate_month[None, :]
    sched = held * sched_rate[None, :]
    lost = mdr * held
    prepaid = smm * (held - sched - lost)
    principal = sched + prepaid + lost
    return (held - principal, principal, interest)


def priority_mask(tranche_order):
    count = tranche_order.shape[1]
    spots = jnp.arange(count, dtype=jnp.int32)
    hits = tranche_order[:, :, None] == spots[None, None, :]
    prio = jnp.sum(jnp.where(hits, spots[None, :, None], 0), axis=1)
    return (prio[:, :, None] < prio[:, None, :]).astype(jnp.float32)


def waterfall(princ, inter, starts, shares, rates, ahead_mask, short, valid):
    steps = princ.shape[2]
    blank = 1.0 - valid
    weights = shares / (jnp.sum(shares, axis=1, keepdims=True) + blank[:, None])
    opening = weights * starts[:, None]
    safe_open = opening + blank[:, None]
    held = jnp.broadcast_to(opening[:, None, :], (princ.shape[0], princ.shape[1], shares.shape[1]))
    decay = jnp.exp(-jnp.cumsum(short + oas_spread, axis=0) / 12.0)
    worth = jnp.zeros_like(held)
    for step in range(steps):
        ahead = jnp.einsum("xpj,xjk->xpk", held, ahead_mask, precision=lax.Precision.HIGHEST)
        paid = jnp.minimum(jnp.maximum(princ[:, :, step, None] - ahead, 0.0), held)
        coupon_due = rates[:, None, :] * held
        denom = jnp.sum(coupon_due, axis=2, keepdims=True) + blank[:, None, None]
        flow = paid + inter[:, :, step, None] * coupon_due / denom
        worth = worth + flow * decay[step][None, :, None]
        held = held - paid
    worth = worth + held * decay[steps - 1][None, :, None]
    return jnp.sum(worth / safe_open[:, None, :], axis=1)


def on_device(
    loan_features,
    hazard_coef,
    coupon,
    balance,
    loan_term,
    loan_age,
    loan_region,
    loan_deal,
    region_hpi,
    rate_paths,
    deal_owner,
    tranche_order,
    tranche_share,
    tranche_rate,
):
    highest = lax.Precision.HIGHEST
    loans_here = coupon.shape[0]
    paths_here = rate_paths.shape[2]
    steps = rate_paths.shape[1]
    deals = deal_owner.shape[0]
    groups = lax.axis_size("loans")
    me_loan = lax.axis_index("loans")
    covar = jnp.dot(loan_features, hazard_coef, preferred_element_type=jnp.float32)
    piece = lax.all_gather(region_hpi, "loans", axis=0, tiled=True)
    rows = piece.shape[0]
    marks = (loan_region[None, :] == lax.iota(jnp.int32, rows)[:, None]).astype(jnp.float32)
    loan_hpi = jnp.einsum("rc,rl->cl", piece.reshape(rows, -1), marks, precision=highest)
    loan_hpi = loan_hpi.reshape(steps, paths_here, loans_here)
    rate_month = coupon / 12.0
    term_left = (loan_term - loan_age).astype(jnp.float32)
    held = jnp.broadcast_to(balance[None, :], (paths_here, loans_here))
    prin_list = []
    int_list = []
    for step in range(steps):
        sched_rate = rate_month / jnp.expm1((term_left - step) * jnp.log1p(rate_month))
        held, principal, interest = loan_month(
            held, covar, coupon, rate_month, sched_rate, rate_paths[1, step], loan_hpi[step]
        )
        prin_list.append(principal)
        int_list.append(interest)
    cash = jnp.stack([jnp.stack(prin_list, 1), jnp.stack(int_list, 1)], 1)
    deal_ids = lax.iota(jnp.int32, deals)
    match = loan_deal[:, None] == deal_ids[None, :]
    onehot_deal = match.astype(jnp.float32)
    totals = lax.psum(jnp.dot(balance, onehot_deal, precision=highest), "loans")
    owners = deal_owner[:, 0]
    order_key = owners * deals + deal_ids
    position = jnp.sum((order_key[None, :] < order_key[:, None]).astype(jnp.int32), axis=1)
    place = (position[None, :] == deal_ids[:, None]).astype(jnp.float32)
    ahead_mask = priority_mask(tranche_order)
    portion = paths_here // groups
    block = cash.reshape(-1, loans_here)
    path_flows = lax.psum_scatter(
        jnp.dot(block, onehot_deal, precision=highest).reshape(
            portion * lax.axis_size("loans"), 2, steps, deals
        ),
        "loans",
        scatter_dimension=0,
        tiled=True,
    )
    flows = path_flows.transpose(3, 0, 1, 2)
    short = lax.dynamic_slice_in_dim(rate_paths[0], me_loan * portion, portion, 1)
    by_deal = waterfall(
        flows[:, :, 0, :],
        flows[:, :, 1, :],
        totals,
        tranche_share,
        tranche_rate,
        ahead_mask,
        short,
        jnp.ones((deals,), jnp.float32),
    )
    ordered = jnp.dot(place, by_deal, precision=highest)
    mine = lax.psum(ordered, "loans")
    total = lax.psum(mine, "paths")
    all_paths = paths_here * lax.axis_size("paths")
    return 100.0 * (total / all_paths - 1.0)


MESH = pl.DeviceIdType.MESH


def rows_of(x):
    return x.reshape((1,) + x.shape)


def pool_kernel(groups, lanes_out,
                feat, coef, coupon, balance, term, age, region, deal, hpi, rates, owner, order, share, trate,
                out,
                loan_tx, loan_rx, hpi_tx, hpi_rx, end_tx, end_rx, left, marks, end_marks, picks, balances, cash, pool, table, cols,
                part, part_rx, half, half_rx,
                loan_ss, loan_rs, hpi_ss, hpi_rs, end_ss, end_rs, part_ss, part_rs, half_ss, half_rs, own_sem):
    n_loans, n_paths = groups
    f32, bf16 = jnp.float32, jnp.bfloat16
    me = lax.axis_index("loans")
    me_path = lax.axis_index("paths")
    n = coupon.shape[1]
    steps, rows, paths = hpi.shape
    here = paths // n_loans
    wide = -(-rows // 128) * 128
    split = end_tx.shape[1]
    deals, tranches = share.shape
    copies = lanes_out // deals

    barrier = pltpu.get_barrier_semaphore()
    for off in range(1, n_loans):
        pl.semaphore_signal(barrier, inc=1, device_id={"loans": lax.rem(me + off, n_loans)}, device_id_type=MESH)
    for off in range(1, n_paths):
        pl.semaphore_signal(barrier, inc=1, device_id={"paths": lax.rem(me_path + off, n_paths)}, device_id_type=MESH)

    covar = lax.dot_general(coef[...], feat[...], (((1,), (1,)), ((), ())), preferred_element_type=f32)
    note = coupon[...]
    place = region[...]
    place = place + (place // rows) * (wide - rows)
    loan_tx[...] = jnp.concatenate(
        [
            0.5 * (covar[0:1, :] + prepay_base + incentive * note),
            0.5 * (covar[1:2, :] + default_base),
            note / 12.0,
            balance[...],
            (term[...] - age[...]).astype(f32),
            place.astype(f32),
            deal[...].astype(f32),
            jnp.zeros((1, n), f32),
        ],
        axis=0,
    )
    pl.semaphore_wait(barrier, n_loans + n_paths - 2)
    loan_copies, hpi_copies, end_copies = [], [], []
    for off in range(1, n_loans):
        there = lax.rem(me + off, n_loans)
        loan_copies.append(pltpu.make_async_remote_copy(
            src_ref=loan_tx, dst_ref=loan_rx.at[me], send_sem=loan_ss.at[off], recv_sem=loan_rs.at[off],
            device_id={"loans": there}, device_id_type=MESH))
        hpi_copies.append(pltpu.make_async_remote_copy(
            src_ref=hpi_tx.at[there], dst_ref=hpi_rx.at[me], send_sem=hpi_ss.at[off], recv_sem=hpi_rs.at[off],
            device_id={"loans": there}, device_id_type=MESH))
        end_copies.append(pltpu.make_async_remote_copy(
            src_ref=end_tx.at[there], dst_ref=end_rx.at[me], send_sem=end_ss.at[off], recv_sem=end_rs.at[off],
            device_id={"loans": there}, device_id_type=MESH))
    for copy in loan_copies:
        copy.start()
    own_loan = pltpu.make_async_copy(loan_tx, loan_rx.at[me], own_sem.at[0])
    own_loan.start()
    blocks = [hpi[step] * (-0.5 * price_sens) for step in range(steps)]
    quarter = lax.broadcasted_iota(jnp.int32, (rows, paths), 1) // here
    for q in range(n_loans):
        packs = None
        for t in range(EARLY):
            x = blocks[t] if t == q else pltpu.roll(blocks[t], ((t - q) % n_loans) * here, 1)
            packs = x if packs is None else jnp.where(quarter == t, x, packs)
        hpi_tx[q] = packs
    for copy in hpi_copies:
        copy.start()
    own_hpi = pltpu.make_async_copy(hpi_tx.at[me], hpi_rx.at[me], own_sem.at[1])
    own_hpi.start()
    pad = jnp.zeros((2 * split - rows, paths), f32)
    for q in range(n_loans):
        packs = None
        for t in range(n_loans):
            x = blocks[EARLY + t % 2]
            x = x[:split] if t < 2 else jnp.concatenate([x[split:], pad], axis=0)
            x = x if t == q else pltpu.roll(x, ((t - q) % n_loans) * here, 1)
            packs = x if packs is None else jnp.where(quarter[:split] == t, x, packs)
        end_tx[q] = packs
    for copy in end_copies:
        copy.start()
    own_end = pltpu.make_async_copy(end_tx.at[me], end_rx.at[me], own_sem.at[2])
    own_end.start()

    key = (jnp.broadcast_to(owner[...], (deals, deals)) * deals
           + lax.broadcasted_iota(jnp.int32, (deals, deals), 1)).astype(f32)
    key_col = jnp.concatenate([key, jnp.zeros((128 - deals, deals), f32)], axis=0).T[:, :deals]
    below = jnp.where(key_col < key, 1.0, 0.0).astype(f32)
    spot = jnp.sum(below, axis=0, keepdims=True)
    perm = jnp.where(spot == lax.broadcasted_iota(jnp.int32, (deals, deals), 0).astype(f32), 1.0, 0.0).astype(f32)
    listing = jnp.sum(perm * lax.broadcasted_iota(jnp.int32, (deals, deals), 1).astype(f32), axis=1, keepdims=True)
    listing = jnp.concatenate([listing] * copies, axis=0)

    def spread(x):
        x = jnp.dot(perm, x, preferred_element_type=f32, precision=lax.Precision.HIGHEST)
        x = jnp.concatenate([x, jnp.zeros((deals, 128 - tranches), f32)], axis=1)
        return jnp.concatenate([x] * copies, axis=0).T[:tranches, :]

    table[...] = spread(order[...].astype(f32))
    share_t = spread(share[...])
    rate_t = spread(trate[...])
    names = lax.broadcasted_iota(jnp.int32, (tranches, lanes_out), 0).astype(f32)

    def walk(j, carry):
        run, upto = carry
        hit = names == table[pl.ds(j, 1), :]
        run = run + jnp.sum(jnp.where(hit, share_t, 0.0), axis=0, keepdims=True)
        return run, jnp.where(hit, run, upto)

    whole, upto = lax.fori_loop(
        0, tranches, walk, (jnp.zeros((1, lanes_out), f32), jnp.zeros((tranches, lanes_out), f32)), unroll=4)
    weight = share_t / whole
    upto = upto / whole
    per_weight = 1.0 / weight
    due_t = rate_t * weight

    stack = jnp.concatenate([rates[t] for t in range(steps)] + [jnp.zeros((128 - 2 * steps, paths), f32)], axis=0)
    cols[...] = stack.T
    mine = cols[pl.ds(pl.multiple_of(me * here, here), here), :]
    mort = [(0.5 * incentive) * mine[:, 2 * t + 1:2 * t + 2] for t in range(steps)]
    disc = []
    total = jnp.zeros((here, 1), f32)
    for t in range(steps):
        total = total + (mine[:, 2 * t:2 * t + 1] + oas_spread)
        disc.append(jnp.exp(-total / 12.0))

    own_loan.wait()
    for copy in loan_copies:
        copy.wait_recv()
    ages = lax.broadcasted_iota(jnp.int32, (8, n), 0).astype(f32)
    for src in range(n_loans):
        r = loan_rx[src, 2:3, :]
        grown = 1.0 + r
        log = jnp.log(grown) * (r / (grown - 1.0))
        x = (loan_rx[src, 4:5, :] - ages) * log
        left[src] = r / (jnp.exp(x) - 1.0)
    pool[...] = jnp.zeros(pool.shape, f32)
    own_hpi.wait()
    for copy in hpi_copies:
        copy.wait_recv()
    height = EARLY * here
    tail = (steps - EARLY) * here
    for src in range(n_loans):
        x = hpi_rx[src]
        if wide > rows:
            x = jnp.concatenate([x, jnp.zeros((wide - rows, paths), f32)], axis=0)
        x = x.T
        high = x.astype(bf16)
        marks[0:height, src * wide:(src + 1) * wide] = high
        marks[height:2 * height, src * wide:(src + 1) * wide] = (x - high.astype(f32)).astype(bf16)

    depth = n_loans * wide

    def months(got, held, lv, sched_rate, first, last, size):
        r = lv[2:3, :]
        for t in range(first, last):
            k = t - first
            h = got[k * here:(k + 1) * here] + got[size + k * here:size + (k + 1) * here]
            smm = 0.5 + 0.5 * jnp.tanh(lv[0:1, :] - mort[t])
            mdr = 0.5 + 0.5 * jnp.tanh(lv[1:2, :] + h)
            interest = held * r
            sched = held * sched_rate[t:t + 1, :]
            lost = mdr * held
            principal = sched + smm * (held - sched - lost) + lost
            held = held - principal
            base = k * 4 * here
            for k, x in enumerate((principal, interest)):
                high = x.astype(bf16)
                cash[base + k * here:base + (k + 1) * here, :] = high
                cash[base + (k + 2) * here:base + (k + 3) * here, :] = (x - high.astype(f32)).astype(bf16)
        return held

    def early(src, _):
        lv = loan_rx[src]
        pick = jnp.where(
            lax.broadcasted_iota(jnp.int32, (depth, n), 0) == lv[5:6, :].astype(jnp.int32), 1.0, 0.0).astype(bf16)
        picks[src] = pick
        got = jnp.dot(marks[...], pick, preferred_element_type=f32)
        held = months(got, jnp.broadcast_to(lv[3:4, :], (here, n)), lv, left[src], 0, EARLY, height)
        balances[src] = held
        b = jnp.broadcast_to(lv[3:4, :], (16, n))
        high = b.astype(bf16)
        cash[4 * height:4 * height + 16, :] = high
        cash[4 * height + 16:4 * height + 32, :] = (b - high.astype(f32)).astype(bf16)
        member = jnp.where(listing == lv[6:7, :], 1.0, 0.0).astype(bf16)
        pool[0:4 * height + 32, :] += lax.dot_general(
            cash[...], member, (((1,), (1,)), ((), ())), preferred_element_type=f32)
        return 0

    lax.fori_loop(0, n_loans, early, 0)

    own_end.wait()
    for copy in end_copies:
        copy.wait_recv()
    for src in range(n_loans):
        x = jnp.concatenate([end_rx[src], jnp.zeros((128 - split, paths), f32)], axis=0).T
        upper = pltpu.roll(x[tail:], split, 1)
        x = jnp.where(lax.broadcasted_iota(jnp.int32, (tail, wide), 1) < split, x[:tail], upper)
        high = x.astype(bf16)
        end_marks[0:tail, src * wide:(src + 1) * wide] = high
        end_marks[tail:2 * tail, src * wide:(src + 1) * wide] = (x - high.astype(f32)).astype(bf16)

    def late(src, _):
        lv = loan_rx[src]
        got = jnp.dot(end_marks[...], picks[src], preferred_element_type=f32)
        months(got, balances[src], lv, left[src], EARLY, steps, tail)
        member = jnp.where(listing == lv[6:7, :], 1.0, 0.0).astype(bf16)
        pool[4 * height + 32:, :] += lax.dot_general(
            cash[0:4 * tail, :], member, (((1,), (1,)), ((), ())), preferred_element_type=f32)
        return 0

    lax.fori_loop(0, n_loans, late, 0)

    start = pool[4 * height:4 * height + 1, :] + pool[4 * height + 16:4 * height + 17, :]
    per_start = 1.0 / start
    sub = here // copies
    group = lax.broadcasted_iota(jnp.int32, (sub, lanes_out), 1) // deals

    def packed(x):
        x = jnp.broadcast_to(x, (here, lanes_out))
        y = x[0:sub]
        for c in range(1, copies):
            y = jnp.where(group == c, x[c * sub:(c + 1) * sub], y)
        return y

    paid_upto = jnp.zeros((sub, lanes_out), f32)
    gone, gains, fall = [], [], []
    for t in range(steps):
        base = t * 4 * here + (32 if t >= EARLY else 0)
        princ = packed(pool[base:base + here, :] + pool[base + 2 * here:base + 3 * here, :])
        inter = packed(pool[base + here:base + 2 * here, :] + pool[base + 3 * here:base + 4 * here, :])
        paid_upto = paid_upto + jnp.maximum(princ, 0.0)
        gone.append(paid_upto * per_start)
        gains.append(inter * per_start)
        fall.append(packed(disc[t]))
    worth = jnp.zeros((tranches, lanes_out), f32)
    for j in range(sub):
        frac = jnp.ones((tranches, lanes_out), f32)
        for t in range(steps):
            d = fall[t][j:j + 1, :]
            later = jnp.clip((upto - gone[t][j:j + 1, :]) * per_weight, 0.0, 1.0)
            denom = jnp.sum(due_t * frac, axis=0, keepdims=True)
            flow = (frac - later) + (gains[t][j:j + 1, :] / denom) * (rate_t * frac)
            worth = worth + flow * d
            frac = later
        worth = worth + frac * d
    wt = jnp.concatenate([worth, jnp.zeros((128 - tranches, lanes_out), f32)], axis=0).T
    acc = wt[0:deals]
    low = lax.broadcasted_iota(jnp.int32, (deals // 2, 128), 1) < 64
    for c in range(1, copies):
        acc = acc + wt[c * deals:(c + 1) * deals]
    acc = jnp.where(low, acc[:deals // 2], pltpu.roll(acc[deals // 2:], 64, 1))
    part[...] = acc
    part_copies = []
    for off in range(1, n_loans):
        part_copies.append(pltpu.make_async_remote_copy(
            src_ref=part, dst_ref=part_rx.at[me], send_sem=part_ss.at[off], recv_sem=part_rs.at[off],
            device_id={"loans": lax.rem(me + off, n_loans)}, device_id_type=MESH))
    for copy in part_copies:
        copy.start()
    part_rx[me] = acc
    for copy in part_copies:
        copy.wait_recv()
    acc = part_rx[0]
    for src in range(1, n_loans):
        acc = acc + part_rx[src]
    half[...] = acc
    half_copies = []
    for off in range(1, n_paths):
        half_copies.append(pltpu.make_async_remote_copy(
            src_ref=half, dst_ref=half_rx.at[me_path], send_sem=half_ss.at[off], recv_sem=half_rs.at[off],
            device_id={"paths": lax.rem(me_path + off, n_paths)}, device_id_type=MESH))
    for copy in half_copies:
        copy.start()
    half_rx[me_path] = acc
    for copy in half_copies:
        copy.wait_recv()
    acc = half_rx[0]
    for src in range(1, n_paths):
        acc = acc + half_rx[src]
    acc = 100.0 * (acc / (paths * n_paths) - 1.0)
    out[:deals // 2, :] = acc[:, :tranches]
    out[deals // 2:, :] = pltpu.roll(acc, 64, 1)[:, :tranches]
    for copy in loan_copies + hpi_copies + end_copies + part_copies + half_copies:
        copy.wait_send()


def fused(loan_features, hazard_coef, coupon, balance, loan_term, loan_age, loan_region, loan_deal,
          region_hpi, rate_paths, deal_owner, tranche_order, tranche_share, tranche_rate):
    n_loans, n_paths = lax.axis_size("loans"), lax.axis_size("paths")
    n = coupon.shape[0]
    rows, steps, paths = region_hpi.shape
    deals, tranches = tranche_share.shape
    here = paths // n_loans
    wide = -(-rows // 128) * 128
    lanes_out = 128
    split = -(-rows // 16) * 8
    height = steps * here
    f32 = jnp.float32
    dma = pltpu.SemaphoreType.DMA
    return pl.pallas_call(
        functools.partial(pool_kernel, (n_loans, n_paths), lanes_out),
        out_shape=jax.ShapeDtypeStruct((deals, tranches), f32),
        in_specs=[pl.BlockSpec(memory_space=pltpu.VMEM)] * 14,
        out_specs=pl.BlockSpec(memory_space=pltpu.VMEM),
        scratch_shapes=[
            pltpu.VMEM((8, n), f32),
            pltpu.VMEM((n_loans, 8, n), f32),
            pltpu.VMEM((n_loans, rows, paths), f32),
            pltpu.VMEM((n_loans, rows, paths), f32),
            pltpu.VMEM((n_loans, split, paths), f32),
            pltpu.VMEM((n_loans, split, paths), f32),
            pltpu.VMEM((n_loans, 8, n), f32),
            pltpu.VMEM((2 * EARLY * here, n_loans * wide), jnp.bfloat16),
            pltpu.VMEM((2 * (steps - EARLY) * here, n_loans * wide), jnp.bfloat16),
            pltpu.VMEM((n_loans, n_loans * wide, n), jnp.bfloat16),
            pltpu.VMEM((n_loans, here, n), f32),
            pltpu.VMEM((4 * EARLY * here + 32, n), jnp.bfloat16),
            pltpu.VMEM((4 * height + 32, lanes_out), f32),
            pltpu.VMEM((tranches, lanes_out), f32),
            pltpu.VMEM((paths, 128), f32),
            pltpu.VMEM((deals // 2, 128), f32),
            pltpu.VMEM((n_loans, deals // 2, 128), f32),
            pltpu.VMEM((deals // 2, 128), f32),
            pltpu.VMEM((n_paths, deals // 2, 128), f32),
            dma((n_loans,)), dma((n_loans,)), dma((n_loans,)), dma((n_loans,)),
            dma((n_loans,)), dma((n_loans,)), dma((n_loans,)), dma((n_loans,)),
            dma((n_paths,)), dma((n_paths,)), dma((3,)),
        ],
        compiler_params=pltpu.CompilerParams(collective_id=0, has_side_effects=True),
    )(loan_features, hazard_coef.T, rows_of(coupon), rows_of(balance), rows_of(loan_term), rows_of(loan_age),
      rows_of(loan_region), rows_of(loan_deal), region_hpi.transpose(1, 0, 2),
      rate_paths.transpose(1, 0, 2), deal_owner.reshape(1, deals), tranche_order, tranche_share, tranche_rate)


def fits(args):
    n = args[2].shape[0]
    paths = args[8].shape[2]
    deals, tranches = args[12].shape
    n_loans = lax.axis_size("loans")
    rows, steps = args[8].shape[:2]
    return (
        paths == 128 and n_loans == EARLY and steps == EARLY + 2 and rows % 8 == 0 and 64 < rows <= 128
        and deals % 16 == 0 and 128 % deals == 0 and tranches == 64
        and (paths // n_loans) % (8 * (128 // deals)) == 0 and n % 128 == 0 and n <= 2048
    )


def device_program(*args):
    return fused(*args) if fits(args) else on_device(*args)


def solution(mesh):
    in_specs = (
        P(("groups", "loans"), None),
        P(),
        P(("groups", "loans")),
        P(("groups", "loans")),
        P(("groups", "loans")),
        P(("groups", "loans")),
        P(("groups", "loans")),
        P(("groups", "loans")),
        P(("groups", "loans"), None, "paths"),
        P(None, None, ("groups", "paths")),
        P("groups", None),
        P("groups", None),
        P("groups", None),
        P("groups", None),
    )
    out_specs = P("groups", None)
    return jax.shard_map(
        device_program, mesh=mesh, in_specs=in_specs, out_specs=out_specs, check_vma=False
    )
```

```python
import functools

import jax
import jax.numpy as jnp
from jax import lax
from jax.experimental import pallas as pl
from jax.experimental.pallas import tpu as pltpu
from jax.sharding import PartitionSpec as P

prepay_base = -4.0
incentive = 40.0
default_base = -6.0
price_sens = 12.0
oas_spread = 0.005
SPAN = 2


def loan_month(held, covar, coupon, rate_month, sched_rate, mortgage_now, hpi_now):
    smm = jax.nn.sigmoid(
        covar[:, 0][None, :] + prepay_base + incentive * (coupon[None, :] - mortgage_now[:, None])
    )
    mdr = jax.nn.sigmoid(covar[:, 1][None, :] + default_base - price_sens * hpi_now)
    interest = held * rate_month[None, :]
    sched = held * sched_rate[None, :]
    lost = mdr * held
    prepaid = smm * (held - sched - lost)
    principal = sched + prepaid + lost
    return (held - principal, principal, interest)


def priority_mask(tranche_order):
    count = tranche_order.shape[1]
    spots = jnp.arange(count, dtype=jnp.int32)
    hits = tranche_order[:, :, None] == spots[None, None, :]
    prio = jnp.sum(jnp.where(hits, spots[None, :, None], 0), axis=1)
    return (prio[:, :, None] < prio[:, None, :]).astype(jnp.float32)


def waterfall(princ, inter, starts, shares, rates, ahead_mask, short, valid):
    steps = princ.shape[2]
    blank = 1.0 - valid
    weights = shares / (jnp.sum(shares, axis=1, keepdims=True) + blank[:, None])
    opening = weights * starts[:, None]
    safe_open = opening + blank[:, None]
    held = jnp.broadcast_to(opening[:, None, :], (princ.shape[0], princ.shape[1], shares.shape[1]))
    decay = jnp.exp(-jnp.cumsum(short + oas_spread, axis=0) / 12.0)
    worth = jnp.zeros_like(held)
    for step in range(steps):
        ahead = jnp.einsum("xpj,xjk->xpk", held, ahead_mask, precision=lax.Precision.HIGHEST)
        paid = jnp.minimum(jnp.maximum(princ[:, :, step, None] - ahead, 0.0), held)
        coupon_due = rates[:, None, :] * held
        denom = jnp.sum(coupon_due, axis=2, keepdims=True) + blank[:, None, None]
        flow = paid + inter[:, :, step, None] * coupon_due / denom
        worth = worth + flow * decay[step][None, :, None]
        held = held - paid
    worth = worth + held * decay[steps - 1][None, :, None]
    return jnp.sum(worth / safe_open[:, None, :], axis=1)


def on_device(
    loan_features,
    hazard_coef,
    coupon,
    balance,
    loan_term,
    loan_age,
    loan_region,
    loan_deal,
    region_hpi,
    rate_paths,
    deal_owner,
    tranche_order,
    tranche_share,
    tranche_rate,
):
    highest = lax.Precision.HIGHEST
    loans_here = coupon.shape[0]
    paths_here = rate_paths.shape[2]
    steps = rate_paths.shape[1]
    deals = deal_owner.shape[0]
    groups = lax.axis_size("loans")
    me_loan = lax.axis_index("loans")
    covar = jnp.dot(loan_features, hazard_coef, preferred_element_type=jnp.float32)
    piece = lax.all_gather(region_hpi, "loans", axis=0, tiled=True)
    rows = piece.shape[0]
    marks = (loan_region[None, :] == lax.iota(jnp.int32, rows)[:, None]).astype(jnp.float32)
    loan_hpi = jnp.einsum("rc,rl->cl", piece.reshape(rows, -1), marks, precision=highest)
    loan_hpi = loan_hpi.reshape(steps, paths_here, loans_here)
    rate_month = coupon / 12.0
    term_left = (loan_term - loan_age).astype(jnp.float32)
    held = jnp.broadcast_to(balance[None, :], (paths_here, loans_here))
    prin_list = []
    int_list = []
    for step in range(steps):
        sched_rate = rate_month / jnp.expm1((term_left - step) * jnp.log1p(rate_month))
        held, principal, interest = loan_month(
            held, covar, coupon, rate_month, sched_rate, rate_paths[1, step], loan_hpi[step]
        )
        prin_list.append(principal)
        int_list.append(interest)
    cash = jnp.stack([jnp.stack(prin_list, 1), jnp.stack(int_list, 1)], 1)
    deal_ids = lax.iota(jnp.int32, deals)
    match = loan_deal[:, None] == deal_ids[None, :]
    onehot_deal = match.astype(jnp.float32)
    totals = lax.psum(jnp.dot(balance, onehot_deal, precision=highest), "loans")
    owners = deal_owner[:, 0]
    order_key = owners * deals + deal_ids
    position = jnp.sum((order_key[None, :] < order_key[:, None]).astype(jnp.int32), axis=1)
    place = (position[None, :] == deal_ids[:, None]).astype(jnp.float32)
    ahead_mask = priority_mask(tranche_order)
    portion = paths_here // groups
    block = cash.reshape(-1, loans_here)
    path_flows = lax.psum_scatter(
        jnp.dot(block, onehot_deal, precision=highest).reshape(
            portion * lax.axis_size("loans"), 2, steps, deals
        ),
        "loans",
        scatter_dimension=0,
        tiled=True,
    )
    flows = path_flows.transpose(3, 0, 1, 2)
    short = lax.dynamic_slice_in_dim(rate_paths[0], me_loan * portion, portion, 1)
    by_deal = waterfall(
        flows[:, :, 0, :],
        flows[:, :, 1, :],
        totals,
        tranche_share,
        tranche_rate,
        ahead_mask,
        short,
        jnp.ones((deals,), jnp.float32),
    )
    ordered = jnp.dot(place, by_deal, precision=highest)
    mine = lax.psum(ordered, "loans")
    total = lax.psum(mine, "paths")
    all_paths = paths_here * lax.axis_size("paths")
    return 100.0 * (total / all_paths - 1.0)


MESH = pl.DeviceIdType.MESH


def rows_of(x):
    return x.reshape((1,) + x.shape)


def pool_kernel(groups, lanes_out,
                feat, coef, coupon, balance, term, age, region, deal, hpi, rates, owner, order, share, trate,
                out,
                loan_tx, loan_rx, hpi_tx, hpi_rx, left, marks, picks, members, balances, cash, pool, table, cols,
                part, part_rx, half, half_rx,
                loan_ss, loan_rs, pass_ss, pass_rs, hpi_ss, hpi_rs, part_ss, part_rs, half_ss, half_rs, own_sem):
    n_loans, n_paths = groups
    f32, bf16 = jnp.float32, jnp.bfloat16
    me = lax.axis_index("loans")
    me_path = lax.axis_index("paths")
    n = coupon.shape[1]
    steps, rows, paths = hpi.shape
    here = paths // n_loans
    wide = -(-rows // 128) * 128
    split = hpi_tx.shape[2]
    spans = steps // SPAN
    deals, tranches = share.shape
    copies = lanes_out // deals

    barrier = pltpu.get_barrier_semaphore()
    for off in range(1, n_loans):
        pl.semaphore_signal(barrier, inc=1, device_id={"loans": lax.rem(me + off, n_loans)}, device_id_type=MESH)
    for off in range(1, n_paths):
        pl.semaphore_signal(barrier, inc=1, device_id={"paths": lax.rem(me_path + off, n_paths)}, device_id_type=MESH)

    covar = lax.dot_general(coef[...], feat[...], (((1,), (1,)), ((), ())), preferred_element_type=f32)
    note = coupon[...]
    place = region[...]
    place = place + (place // rows) * (wide - rows)
    bundle = jnp.concatenate(
        [
            0.5 * (covar[0:1, :] + prepay_base + incentive * note),
            0.5 * (covar[1:2, :] + default_base),
            note / 12.0,
            balance[...],
            (term[...] - age[...]).astype(f32),
            place.astype(f32),
            deal[...].astype(f32),
            jnp.zeros((1, n), f32),
        ],
        axis=0,
    )
    share_n = n // n_paths
    for q in range(n_paths):
        loan_tx[q] = bundle[:, q * share_n:(q + 1) * share_n]
    pl.semaphore_wait(barrier, n_loans + n_paths - 2)
    loan_copies, pass_copies, hpi_copies = [], [], [[] for _ in range(spans)]
    for off in range(1, n_loans):
        there, source = lax.rem(me + off, n_loans), lax.rem(me + n_loans - off, n_loans)
        loan_copies.append(pltpu.make_async_remote_copy(
            src_ref=loan_tx.at[me_path], dst_ref=loan_rx.at[me, me_path], send_sem=loan_ss.at[off],
            recv_sem=loan_rs.at[off], device_id={"loans": there}, device_id_type=MESH))
        for hop in range(1, n_paths):
            pass_copies.append(pltpu.make_async_remote_copy(
                src_ref=loan_rx.at[source, me_path], dst_ref=loan_rx.at[source, me_path],
                send_sem=pass_ss.at[off, hop], recv_sem=pass_rs.at[off, hop],
                device_id={"paths": lax.rem(me_path + hop, n_paths)}, device_id_type=MESH))
        for p in range(spans):
            hpi_copies[p].append(pltpu.make_async_remote_copy(
                src_ref=hpi_tx.at[p, there], dst_ref=hpi_rx.at[p, me], send_sem=hpi_ss.at[p, off],
                recv_sem=hpi_rs.at[p, off], device_id={"loans": there}, device_id_type=MESH))
    for copy in loan_copies:
        copy.start()
    own_loan = pltpu.make_async_copy(loan_tx, loan_rx.at[me], own_sem.at[spans])
    own_loan.start()
    quarter = lax.broadcasted_iota(jnp.int32, (split, paths), 1) // here
    pad = jnp.zeros((2 * split - rows, paths), f32)
    own_hpi = []
    for p in range(spans):
        blocks = []
        for t in range(SPAN):
            blocks.append(hpi[SPAN * p + t, 0:split, :] * (-0.5 * price_sens))
        for t in range(SPAN):
            blocks.append(jnp.concatenate([hpi[SPAN * p + t, split:rows, :] * (-0.5 * price_sens), pad], axis=0))
        for q in range(n_loans):
            packs = None
            for t in range(n_loans):
                x = blocks[t] if t == q else pltpu.roll(blocks[t], ((t - q) % n_loans) * here, 1)
                packs = x if packs is None else jnp.where(quarter == t, x, packs)
            hpi_tx[p, q] = packs
        for copy in hpi_copies[p]:
            copy.start()
        own_hpi.append(pltpu.make_async_copy(hpi_tx.at[p, me], hpi_rx.at[p, me], own_sem.at[p]))
        own_hpi[p].start()

    key = (jnp.broadcast_to(owner[...], (deals, deals)) * deals
           + lax.broadcasted_iota(jnp.int32, (deals, deals), 1)).astype(f32)
    key_col = jnp.concatenate([key, jnp.zeros((128 - deals, deals), f32)], axis=0).T[:, :deals]
    below = jnp.where(key_col < key, 1.0, 0.0).astype(f32)
    spot = jnp.sum(below, axis=0, keepdims=True)
    perm = jnp.where(spot == lax.broadcasted_iota(jnp.int32, (deals, deals), 0).astype(f32), 1.0, 0.0).astype(f32)
    listing = jnp.sum(perm * lax.broadcasted_iota(jnp.int32, (deals, deals), 1).astype(f32), axis=1, keepdims=True)

    def spread(x):
        x = jnp.dot(perm, x, preferred_element_type=f32, precision=lax.Precision.HIGHEST)
        x = jnp.concatenate([x, jnp.zeros((deals, 128 - tranches), f32)], axis=1)
        return jnp.concatenate([x] * copies, axis=0).T[:tranches, :]

    table[...] = spread(order[...].astype(f32))
    share_t = spread(share[...])
    rate_t = spread(trate[...])
    names = lax.broadcasted_iota(jnp.int32, (tranches, lanes_out), 0).astype(f32)

    def walk(j, carry):
        run, upto = carry
        hit = names == table[pl.ds(j, 1), :]
        run = run + jnp.sum(jnp.where(hit, share_t, 0.0), axis=0, keepdims=True)
        return run, jnp.where(hit, run, upto)

    whole, upto = lax.fori_loop(
        0, tranches, walk, (jnp.zeros((1, lanes_out), f32), jnp.zeros((tranches, lanes_out), f32)), unroll=4)
    weight = share_t / whole
    upto = upto / whole
    per_weight = 1.0 / weight
    due_t = rate_t * weight

    stack = jnp.concatenate([rates[t] for t in range(steps)] + [jnp.zeros((128 - 2 * steps, paths), f32)], axis=0)
    cols[...] = stack.T
    mine = cols[pl.ds(pl.multiple_of(me * here, here), here), :]
    mort = [(0.5 * incentive) * mine[:, 2 * t + 1:2 * t + 2] for t in range(steps)]
    disc = []
    total = jnp.zeros((here, 1), f32)
    for t in range(steps):
        total = total + (mine[:, 2 * t:2 * t + 1] + oas_spread)
        disc.append(jnp.exp(-total / 12.0))

    own_loan.wait()
    for k, copy in enumerate(loan_copies):
        copy.wait_recv()
        for again in pass_copies[k * (n_paths - 1):(k + 1) * (n_paths - 1)]:
            again.start()
    for copy in pass_copies:
        copy.wait_recv()
    ages = lax.broadcasted_iota(jnp.int32, (8, n), 0).astype(f32)
    depth = n_loans * wide
    tail = SPAN * here
    base_sums = jnp.zeros((32, lanes_out), f32)
    for src in range(n_loans):
        lv = jnp.concatenate([loan_rx[src, q] for q in range(n_paths)], axis=1)
        r = lv[2:3, :]
        grown = 1.0 + r
        log = jnp.log(grown) * (r / (grown - 1.0))
        x = (lv[4:5, :] - ages) * log
        left[src] = r / (jnp.exp(x) - 1.0)
        picks[src] = jnp.where(
            lax.broadcasted_iota(jnp.int32, (depth, n), 0) == lv[5:6, :].astype(jnp.int32), 1.0, 0.0).astype(bf16)
        hit = listing == lv[6:7, :]
        r_high = r.astype(bf16).astype(f32)
        member = jnp.concatenate(
            [jnp.where(hit, 1.0, 0.0), jnp.where(hit, r_high, 0.0), jnp.where(hit, r - r_high, 0.0),
             jnp.zeros((lanes_out - 3 * deals, n), f32)], axis=0).astype(bf16)
        members[src] = member
        b = jnp.broadcast_to(lv[3:4, :], (16, n))
        high = b.astype(bf16)
        both = jnp.concatenate([high, (b - high.astype(f32)).astype(bf16)], axis=0)
        base_sums = base_sums + lax.dot_general(both, member, (((1,), (1,)), ((), ())), preferred_element_type=f32)

    for p in range(spans):
        own_hpi[p].wait()
        for copy in hpi_copies[p]:
            copy.wait_recv()
        for src in range(n_loans):
            x = jnp.concatenate([hpi_rx[p, src], jnp.zeros((128 - split, paths), f32)], axis=0).T
            upper = pltpu.roll(x[tail:], split, 1)
            x = jnp.where(lax.broadcasted_iota(jnp.int32, (tail, wide), 1) < split, x[:tail], upper)
            high = x.astype(bf16)
            marks[p, 0:tail, src * wide:(src + 1) * wide] = high
            marks[p, tail:2 * tail, src * wide:(src + 1) * wide] = (x - high.astype(f32)).astype(bf16)
        sums = jnp.zeros((2 * tail, lanes_out), f32)
        for src in range(n_loans):
            lv = jnp.concatenate([loan_rx[src, q] for q in range(n_paths)], axis=1)
            got = jnp.dot(marks[p], picks[src], preferred_element_type=f32)
            held = jnp.broadcast_to(lv[3:4, :], (here, n)) if p == 0 else balances[src]
            for t in range(SPAN):
                h = got[t * here:(t + 1) * here] + got[tail + t * here:tail + (t + 1) * here]
                smm = 0.5 + 0.5 * jnp.tanh(lv[0:1, :] - mort[SPAN * p + t])
                mdr = 0.5 + 0.5 * jnp.tanh(lv[1:2, :] + h)
                sched = held * left[src, SPAN * p + t:SPAN * p + t + 1, :]
                lost = mdr * held
                principal = sched + smm * (held - sched - lost) + lost
                held = held - principal
                high = principal.astype(bf16)
                cash[src % 2, t * here:(t + 1) * here, :] = high
                cash[src % 2, tail + t * here:tail + (t + 1) * here, :] = (
                    principal - high.astype(f32)).astype(bf16)
            if p < spans - 1:
                balances[src] = held
            sums = sums + lax.dot_general(
                cash[src % 2], members[src], (((1,), (1,)), ((), ())), preferred_element_type=f32)
        pool[p * tail:(p + 1) * tail, :] = sums[:tail] + sums[tail:]

    sub = here // copies
    group = lax.broadcasted_iota(jnp.int32, (sub, lanes_out), 1) // deals

    def packed(x):
        x = jnp.broadcast_to(x, (here, lanes_out))
        y = x[0:sub]
        for c in range(1, copies):
            y = jnp.where(group == c, x[c * sub:(c + 1) * sub], y)
        return y

    def shifted(x, column):
        pieces = [x[c * sub:(c + 1) * sub] for c in range(copies)]
        turned = [pltpu.roll(y, ((c - column) % copies) * deals, 1) if (c - column) % copies else y
                  for c, y in enumerate(pieces)]
        y = turned[0]
        for c in range(1, copies):
            y = jnp.where(group == c, turned[c], y)
        return y

    bases = jnp.concatenate([base_sums[0:sub] + base_sums[16:16 + sub]] * copies, axis=0)
    per_start = 1.0 / shifted(bases, 0)
    inter = shifted(bases, 1) + shifted(bases, 2)
    paid_upto = jnp.zeros((sub, lanes_out), f32)
    gone, gains, fall = [], [], []
    for t in range(steps):
        x = pool[t * here:(t + 1) * here, :]
        paid_upto = paid_upto + jnp.maximum(shifted(x, 0), 0.0)
        gone.append(paid_upto * per_start)
        gains.append(inter * per_start)
        inter = inter - (shifted(x, 1) + shifted(x, 2))
        fall.append(packed(disc[t]))
    worth = jnp.zeros((tranches, lanes_out), f32)
    for j in range(sub):
        frac = jnp.ones((tranches, lanes_out), f32)
        for t in range(steps):
            d = fall[t][j:j + 1, :]
            later = jnp.clip((upto - gone[t][j:j + 1, :]) * per_weight, 0.0, 1.0)
            denom = jnp.sum(due_t * frac, axis=0, keepdims=True)
            flow = (frac - later) + (gains[t][j:j + 1, :] / denom) * (rate_t * frac)
            worth = worth + flow * d
            frac = later
        worth = worth + frac * d
    wt = jnp.concatenate([worth, jnp.zeros((128 - tranches, lanes_out), f32)], axis=0).T
    acc = wt[0:deals]
    low = lax.broadcasted_iota(jnp.int32, (deals // 2, 128), 1) < 64
    for c in range(1, copies):
        acc = acc + wt[c * deals:(c + 1) * deals]
    acc = jnp.where(low, acc[:deals // 2], pltpu.roll(acc[deals // 2:], 64, 1))
    part[...] = acc
    part_copies = []
    for off in range(1, n_loans):
        part_copies.append(pltpu.make_async_remote_copy(
            src_ref=part, dst_ref=part_rx.at[me], send_sem=part_ss.at[off], recv_sem=part_rs.at[off],
            device_id={"loans": lax.rem(me + off, n_loans)}, device_id_type=MESH))
    for copy in part_copies:
        copy.start()
    part_rx[me] = acc
    for copy in part_copies:
        copy.wait_recv()
    acc = part_rx[0]
    for src in range(1, n_loans):
        acc = acc + part_rx[src]
    half[...] = acc
    half_copies = []
    for off in range(1, n_paths):
        half_copies.append(pltpu.make_async_remote_copy(
            src_ref=half, dst_ref=half_rx.at[me_path], send_sem=half_ss.at[off], recv_sem=half_rs.at[off],
            device_id={"paths": lax.rem(me_path + off, n_paths)}, device_id_type=MESH))
    for copy in half_copies:
        copy.start()
    half_rx[me_path] = acc
    for copy in half_copies:
        copy.wait_recv()
    acc = half_rx[0]
    for src in range(1, n_paths):
        acc = acc + half_rx[src]
    acc = 100.0 * (acc / (paths * n_paths) - 1.0)
    out[:deals // 2, :] = acc[:, :tranches]
    out[deals // 2:, :] = pltpu.roll(acc, 64, 1)[:, :tranches]
    for copy in loan_copies + pass_copies + sum(hpi_copies, []) + part_copies + half_copies:
        copy.wait_send()


def fused(loan_features, hazard_coef, coupon, balance, loan_term, loan_age, loan_region, loan_deal,
          region_hpi, rate_paths, deal_owner, tranche_order, tranche_share, tranche_rate):
    n_loans, n_paths = lax.axis_size("loans"), lax.axis_size("paths")
    n = coupon.shape[0]
    rows, steps, paths = region_hpi.shape
    deals, tranches = tranche_share.shape
    here = paths // n_loans
    wide = -(-rows // 128) * 128
    lanes_out = 128
    split = -(-rows // 16) * 8
    height = steps * here
    f32 = jnp.float32
    dma = pltpu.SemaphoreType.DMA
    return pl.pallas_call(
        functools.partial(pool_kernel, (n_loans, n_paths), lanes_out),
        out_shape=jax.ShapeDtypeStruct((deals, tranches), f32),
        in_specs=[pl.BlockSpec(memory_space=pltpu.VMEM)] * 14,
        out_specs=pl.BlockSpec(memory_space=pltpu.VMEM),
        scratch_shapes=[
            pltpu.VMEM((n_paths, 8, n // n_paths), f32),
            pltpu.VMEM((n_loans, n_paths, 8, n // n_paths), f32),
            pltpu.VMEM((steps // SPAN, n_loans, split, paths), f32),
            pltpu.VMEM((steps // SPAN, n_loans, split, paths), f32),
            pltpu.VMEM((n_loans, 8, n), f32),
            pltpu.VMEM((steps // SPAN, 2 * SPAN * here, n_loans * wide), jnp.bfloat16),
            pltpu.VMEM((n_loans, n_loans * wide, n), jnp.bfloat16),
            pltpu.VMEM((n_loans, lanes_out, n), jnp.bfloat16),
            pltpu.VMEM((n_loans, here, n), f32),
            pltpu.VMEM((2, 2 * SPAN * here, n), jnp.bfloat16),
            pltpu.VMEM((height, lanes_out), f32),
            pltpu.VMEM((tranches, lanes_out), f32),
            pltpu.VMEM((paths, 128), f32),
            pltpu.VMEM((deals // 2, 128), f32),
            pltpu.VMEM((n_loans, deals // 2, 128), f32),
            pltpu.VMEM((deals // 2, 128), f32),
            pltpu.VMEM((n_paths, deals // 2, 128), f32),
            dma((n_loans,)), dma((n_loans,)), dma((n_loans, n_paths)), dma((n_loans, n_paths)),
            dma((steps // SPAN, n_loans)), dma((steps // SPAN, n_loans)),
            dma((n_loans,)), dma((n_loans,)), dma((n_paths,)), dma((n_paths,)), dma((steps // SPAN + 1,)),
        ],
        compiler_params=pltpu.CompilerParams(collective_id=0, has_side_effects=True),
    )(loan_features, hazard_coef.T, rows_of(coupon), rows_of(balance), rows_of(loan_term), rows_of(loan_age),
      rows_of(loan_region), rows_of(loan_deal), region_hpi.transpose(1, 0, 2),
      rate_paths.transpose(1, 0, 2), deal_owner.reshape(1, deals), tranche_order, tranche_share, tranche_rate)


def fits(args):
    n = args[2].shape[0]
    paths = args[8].shape[2]
    deals, tranches = args[12].shape
    n_loans = lax.axis_size("loans")
    rows, steps = args[8].shape[:2]
    return (
        paths == 128 and n_loans == 2 * SPAN and steps % SPAN == 0 and steps <= 8 and rows % 8 == 0 and 64 < rows <= 128
        and deals in (16, 32) and tranches == 64
        and (paths // n_loans) % (8 * (128 // deals)) == 0
        and n % (128 * lax.axis_size("paths")) == 0 and n <= 2048
    )


def device_program(*args):
    return fused(*args) if fits(args) else on_device(*args)


def solution(mesh):
    in_specs = (
        P(("groups", "loans"), None),
        P(),
        P(("groups", "loans")),
        P(("groups", "loans")),
        P(("groups", "loans")),
        P(("groups", "loans")),
        P(("groups", "loans")),
        P(("groups", "loans")),
        P(("groups", "loans"), None, "paths"),
        P(None, None, ("groups", "paths")),
        P("groups", None),
        P("groups", None),
        P("groups", None),
        P("groups", None),
    )
    out_specs = P("groups", None)
    return jax.shard_map(
        device_program, mesh=mesh, in_specs=in_specs, out_specs=out_specs, check_vma=False
    )
```
